32 devices in a mesh: prow: 4 (over z), pcol: 8 (over y, x, core).
Axes of the slice: x: 2, y: 2, z: 4, core: 2. Of those that a mesh axis runs over, the one named last changes fastest.
Arguments:
- ainv_in: float32 [36, 4, 18, 8, 128, 128], P(None, 'prow', None, 'pcol'), as said below
- ufactor: bfloat16 [36, 4, 6, 128, 128], P(None, 'prow'), may hold values from -0.08984375 to 0.08984375
- dinv: float32 [6, 128, 128], replicated, may hold values from -6 to 6
- pattern: int32 [144, 144], replicated, may hold values from 0 to 1, as said below
Outputs:
- ainv_out: float32 [36, 4, 18, 8, 128, 128], P(None, 'prow', None, 'pcol')
The draws below stay inside these ranges and needn't reach their ends.
Inputs may be any that keep to these rules, and one draw needn't show every extreme that they name: For a column j below 6, pattern[i, j] is 0 for i <= j, 1 at the parent row (the nearest row below j that has a 1, at most 3 below j), and the other 1s of column j lie in rows where the parent's column has a 1; for j at least 6, pattern[i, j] is 1 exactly where i > j. `ainv_in`: a symmetric matrix.
All inputs are finite; a program needn't handle non-finite values.
Results may differ from the reference program's by a relative error of at most 0.0003.
Values may be sent and summed in bfloat16 or wider, within the bound.
A program may use at most 192 MiB of HBM per device.

```python
import jax
import jax.numpy as jnp
from jax import lax

B = 128
NBLK = 144
NSTEP = 6
RB = 36
CB = 18
N_PROW = 4
N_PCOL = 8


def draw_ainv_in(key, part):
    order = NBLK * B
    noise = jax.random.normal(key, (order, order), jnp.float32)
    symmetric = (noise + noise.T) * (0.7 / (2.0 * order) ** 0.5)
    matrix = symmetric + 2.0 * jnp.eye(order, dtype=jnp.float32)
    return matrix.reshape(RB, NBLK // RB, B, CB, NBLK // CB, B).transpose(0, 1, 3, 4, 2, 5)


def draw_pattern(key, part):
    indices = jnp.arange(NBLK, dtype=jnp.int32)
    initial = ((indices[:, None] > indices[None, :]) & (indices[None, :] >= NSTEP)).astype(jnp.int32)

    def build(taken, current):
        column = NSTEP - 1 - taken
        local_key = jax.random.fold_in(jax.random.fold_in(key, 7), column)
        first_key, second_key = jax.random.split(local_key)
        jump_size = jax.random.randint(first_key, (), 1, 4, dtype=jnp.int32)
        parent = jnp.minimum(column + jump_size, NBLK - 1)
        keep_rows = jax.random.randint(second_key, (NBLK,), 0, 10, dtype=jnp.int32) < 9
        parent_col = lax.dynamic_index_in_dim(current, parent, 1, keepdims=False)
        new_col = (parent_col > 0) & keep_rows | (indices == parent)
        new_col = new_col & (indices > column)
        return lax.dynamic_update_index_in_dim(current, new_col.astype(jnp.int32), column, 1)
    return lax.fori_loop(0, NSTEP, build, initial)


def steps_of(stream_key, extent, shards, smallest, high):
    loudness, own = 1.0, jax.random.fold_in(stream_key, 6)
    for axis_at, shards_of in shards:
        heights = jnp.exp(jax.random.uniform(jax.random.fold_in(own, axis_at), (shards_of,), jnp.float32, smallest / len(shards), high / len(shards)))
        loudness = loudness * jnp.repeat(heights, extent[axis_at] // shards_of).reshape([-1 if axis == axis_at else 1 for axis in range(len(extent))])
    return loudness


def normal_values(stream_key, extent, deviation, reach, cuts=(), kind=jnp.bfloat16):
    drawn = jax.random.normal(stream_key, extent, jnp.float32) * deviation
    if len(cuts) > 0:
        drawn = steps_of(stream_key, extent, cuts, -0.22, 0.18) * drawn
    return jnp.clip(drawn, min=-reach, max=reach).astype(kind)


def setup_inputs(seed: int = 0) -> dict:
    streams_of = jax.random.split(jax.random.key(seed), 5)
    return {
        "ainv_in": draw_ainv_in(jax.random.fold_in(streams_of[4], 71), 0),
        "ufactor": normal_values(streams_of[1], (RB, N_PROW, NSTEP, B, B), 0.015, 0.08984375, ((1, 4),)),
        "dinv": normal_values(streams_of[2], (NSTEP, B, B), 1.0, 6.0, (), jnp.float32),
        "pattern": draw_pattern(jax.random.fold_in(streams_of[4], 71), 0),
    }


def dense_form(blocks):
    return blocks.transpose(0, 1, 4, 2, 3, 5).reshape(NBLK * B, NBLK * B)


def block_form(matrix):
    return matrix.reshape(RB, N_PROW, B, CB, N_PCOL, B).transpose(0, 1, 3, 4, 2, 5)


def reference(ainv_in, ufactor, dinv, pattern):
    matrix = dense_form(ainv_in)
    factor = ufactor.astype(jnp.float32)
    row_mask = jnp.repeat(pattern, B, axis=0).astype(jnp.float32)
    for taken in range(NSTEP):
        column = NSTEP - 1 - taken
        factor_col = factor[:, :, column].reshape(NBLK * B, B) * row_mask[:, column:column + 1]
        inverse_col = -jnp.dot(matrix, factor_col, precision=lax.Precision.HIGHEST) * row_mask[:, column:column + 1]
        diag_block = dinv[column] - jnp.dot(factor_col.T, inverse_col, precision=lax.Precision.HIGHEST)
        new_col = inverse_col.at[column * B:(column + 1) * B].set(diag_block)
        matrix = matrix.at[:, column * B:(column + 1) * B].set(new_col)
        matrix = matrix.at[column * B:(column + 1) * B, :].set(new_col.T)
    return block_form(matrix)
```

```python
import functools

import jax
import jax.numpy as jnp
from jax import lax
from jax.experimental import pallas as pl
from jax.experimental.pallas import tpu as pltpu
from jax.sharding import PartitionSpec as P

F32 = jnp.float32
BF16 = jnp.bfloat16


def largest_divisor(value, most):
    return max(d for d in range(1, most + 1) if value % d == 0)


def pieces(value, count):
    parts = []
    for _ in range(count):
        part = value.astype(BF16)
        parts.append(part)
        value = value - part.astype(F32)
    return parts


def mixed_dot(left, right, dims=(((1,), (0,)), ((), ())), count=3):
    total = None
    for part in reversed(pieces(left, count)):
        term = lax.dot_general(part, right, dims, preferred_element_type=F32)
        total = term if total is None else total + term
    return total


def product_kernel(x_ref, u_ref, o_ref, y_ref, acc_ref):
    k = pl.program_id(1)
    tall, group, width, _ = x_ref.shape
    o_ref[...] = x_ref[...]
    tile = jnp.concatenate([x_ref[:, g].reshape(tall * width, width) for g in range(group)], axis=1)
    high, low = pieces(tile, 2)
    left = u_ref[k]
    part = jnp.dot(left, low, preferred_element_type=F32) + jnp.dot(left, high, preferred_element_type=F32)

    @pl.when(k == 0)
    def _():
        acc_ref[...] = part

    @pl.when(k > 0)
    def _():
        acc_ref[...] += part

    @pl.when(k == pl.num_programs(1) - 1)
    def _():
        y_ref[...] = acc_ref[...].T


def product(blocks, masked, width, steps):
    row_blocks, col_blocks = blocks.shape[:2]
    group = 2 if col_blocks % 2 == 0 else 1
    tall = largest_divisor(row_blocks, 9)
    chunks = row_blocks // tall
    left = masked.reshape(chunks, tall, steps, width, width).transpose(0, 2, 4, 1, 3)
    left = left.reshape(chunks, steps * width, tall * width)
    return pl.pallas_call(
        product_kernel,
        grid=(col_blocks // group, chunks),
        in_specs=[
            pl.BlockSpec((tall, group, width, width), lambda c, k: (k, c, 0, 0)),
            pl.BlockSpec(left.shape, lambda c, k: (0, 0, 0), pipeline_mode=pl.Buffered(1)),
        ],
        out_specs=[
            pl.BlockSpec((tall, group, width, width), lambda c, k: (k, c, 0, 0)),
            pl.BlockSpec((group * width, steps * width), lambda c, k: (c, 0)),
        ],
        out_shape=[
            jax.ShapeDtypeStruct(blocks.shape, F32),
            jax.ShapeDtypeStruct((col_blocks * width, steps * width), F32),
        ],
        scratch_shapes=[pltpu.VMEM((steps * width, group * width), F32)],
        compiler_params=pltpu.CompilerParams(vmem_limit_bytes=56 << 20),
        cost_estimate=pl.CostEstimate(
            flops=4 * row_blocks * col_blocks * width**3 * steps,
            bytes_accessed=8 * row_blocks * col_blocks * width**2,
            transcendentals=0,
        ),
    )(blocks, left)


def substitute_kernel(steps, y_ref, mask_ref, small_ref, rows_ref, z_ref, p_ref):
    width = y_ref.shape[1] // steps
    for k in reversed(range(steps)):
        here = slice(k * width, (k + 1) * width)
        value = y_ref[:, here]
        if k + 1 < steps:
            later = slice((k + 1) * width, steps * width)
            value = value + mixed_dot(z_ref[:, later], small_ref[later, here])
        z_ref[:, here] = jnp.where(mask_ref[:, k : k + 1] > 0, -value, 0.0)
    for j in range(steps):
        upto = slice(0, (j + 1) * width)
        there = slice(j * width, (j + 1) * width)
        if j + 1 < steps:
            p_ref[there, (j + 1) * width :] = jnp.zeros((width, (steps - j - 1) * width), F32)
        p_ref[there, upto] = mixed_dot(z_ref[:, there], rows_ref[:, upto], (((0,), (0,)), ((), ())))


def corner_kernel(steps, p_ref, small_ref, dinv_ref, mask_ref, s_ref):
    width = dinv_ref.shape[1]
    for k in reversed(range(steps)):
        here = slice(k * width, (k + 1) * width)
        diag = dinv_ref[k] - p_ref[here, here].T
        if k + 1 < steps:
            later = slice((k + 1) * width, steps * width)
            factor = small_ref[later, here]
            value = p_ref[later, here] + mixed_dot(s_ref[later, later], factor)
            value = jnp.where(mask_ref[later, k : k + 1] > 0, -value, 0.0)
            diag = diag - mixed_dot(value, factor, (((0,), (0,)), ((), ()))).T
            s_ref[later, here] = value
            s_ref[here, later] = value.T
        s_ref[here, here] = diag.T


def per_device(ainv_in, ufactor, dinv, pattern):
    row_blocks, _, col_blocks, _, width, _ = ainv_in.shape
    steps = dinv.shape[0]
    blocks = ainv_in.reshape(row_blocks, col_blocks, width, width)
    lower = ufactor.reshape(row_blocks, steps, width, width)
    row_count = lax.axis_size("prow")
    col_count = lax.axis_size("pcol")
    prow_id = lax.axis_index("prow")
    pcol_id = lax.axis_index("pcol")
    fold = col_count // row_count
    slots = -(-steps // row_count)
    assert slots <= fold and steps <= col_count
    row_ids = jnp.arange(row_blocks, dtype=jnp.int32) * row_count + prow_id
    col_ids = jnp.arange(col_blocks, dtype=jnp.int32) * col_count + pcol_id

    live = pattern[row_ids, :steps] > 0
    masked = jnp.where(live[:, :, None, None], lower, jnp.zeros_like(lower))
    outer = jnp.where((row_ids >= steps)[:, None, None, None], masked, jnp.zeros_like(masked))

    copied, partial_y = product(blocks, outer, width, steps)

    small = lax.all_gather(masked[:slots], "prow", axis=1)
    small = small.reshape(slots * row_count, steps, width, width)[:steps]
    small = small.transpose(0, 2, 1, 3).reshape(steps * width, steps * width)

    chosen = lax.dynamic_index_in_dim(
        outer.reshape(col_blocks, fold, steps, width, width), pcol_id // row_count, 1, keepdims=False
    )
    chosen = chosen.transpose(0, 2, 1, 3).reshape(col_blocks * width, steps * width)
    chosen = jnp.where(prow_id == pcol_id % row_count, chosen, jnp.zeros_like(chosen))
    factor_rows = lax.psum_scatter(chosen, "prow", scatter_dimension=0, tiled=True)

    share_y = lax.psum_scatter(partial_y, "prow", scatter_dimension=0, tiled=True)
    share = share_y.shape[0]
    mask_cols = jnp.where((col_ids >= steps)[:, None], pattern[col_ids, :steps], 0).astype(F32)
    mask_rows = lax.dynamic_slice_in_dim(jnp.repeat(mask_cols, width, axis=0), prow_id * share, share, 0)

    params = pltpu.CompilerParams(vmem_limit_bytes=40 << 20)
    share_z, products = pl.pallas_call(
        functools.partial(substitute_kernel, steps),
        out_shape=[
            jax.ShapeDtypeStruct(share_y.shape, F32),
            jax.ShapeDtypeStruct((steps * width, steps * width), F32),
        ],
        compiler_params=params,
    )(share_y, mask_rows, small, factor_rows)
    products = lax.psum(products, ("prow", "pcol"))

    mask_small = jnp.repeat(pattern[:steps, :steps].astype(F32), width, axis=0)
    corner = pl.pallas_call(
        functools.partial(corner_kernel, steps),
        out_shape=jax.ShapeDtypeStruct((steps * width, steps * width), F32),
        compiler_params=params,
    )(products, small, dinv, mask_small)
    corner = corner.reshape(steps, width, steps, width)

    padded = jnp.pad(share_z, ((0, 0), (0, (slots * row_count - steps) * width)))
    padded = padded.reshape(share, slots, row_count, width)
    mine = lax.all_to_all(padded, "prow", split_axis=2, concat_axis=0, tiled=True)
    mine = mine.reshape(col_blocks, width, slots, width)

    received = []
    for turn in range(fold):
        pairs = []
        for slot in range(slots):
            side = (turn + slot) % fold
            for p in range(row_count):
                if slot * row_count + p < steps:
                    for r in range(row_count):
                        source = p * col_count + side * row_count + r
                        target = r * col_count + slot * row_count + p
                        pairs.append((source, target))
        slot = jnp.minimum((pcol_id // row_count + fold - turn) % fold, slots - 1)
        payload = lax.dynamic_index_in_dim(mine, slot, 2, keepdims=False)
        received.append(lax.ppermute(payload, ("prow", "pcol"), pairs))
    my_slot = pcol_id // row_count
    stacked = jnp.stack(received)
    new_col = jnp.stack([stacked[(side - my_slot) % fold] for side in range(fold)], axis=1)
    new_col = new_col.reshape(row_blocks, width, width)
    own = jnp.minimum(pcol_id, steps - 1)
    corner_col = lax.dynamic_index_in_dim(corner, own, 2, keepdims=False)
    for slot in range(slots):
        index = slot * row_count + prow_id
        block = lax.dynamic_index_in_dim(corner_col, jnp.minimum(index, steps - 1), 0, keepdims=False)
        new_col = new_col.at[slot].set(jnp.where(index < steps, block, new_col[slot]))
    old_col = copied[:, 0]
    matrix = copied.at[:, 0].set(jnp.where(pcol_id < steps, new_col, old_col))
    for slot in range(slots):
        index = slot * row_count + prow_id
        new_row = jnp.swapaxes(mine[:, :, slot], 1, 2)
        block = lax.dynamic_index_in_dim(corner, jnp.minimum(index, steps - 1), 0, keepdims=False)
        block = lax.dynamic_index_in_dim(block, own, 1, keepdims=False)
        new_row = new_row.at[0].set(jnp.where(pcol_id < steps, block, new_row[0]))
        matrix = matrix.at[slot].set(jnp.where(index < steps, new_row, matrix[slot]))
    return matrix.reshape(ainv_in.shape)


def solution(mesh):
    placed = (
        P(None, "prow", None, "pcol", None, None),
        P(None, "prow", None, None, None),
        P(),
        P(),
    )
    return jax.shard_map(
        per_device,
        mesh=mesh,
        in_specs=placed,
        out_specs=P(None, "prow", None, "pcol", None, None),
        check_vma=False,
    )
```

```python
import functools

import jax
import jax.numpy as jnp
from jax import lax
from jax.experimental import pallas as pl
from jax.experimental.pallas import tpu as pltpu
from jax.sharding import PartitionSpec as P

F32 = jnp.float32
BF16 = jnp.bfloat16


def largest_divisor(value, most):
    return max(d for d in range(1, most + 1) if value % d == 0)


def pieces(value, count):
    parts = []
    for _ in range(count):
        part = value.astype(BF16)
        parts.append(part)
        value = value - part.astype(F32)
    return parts


def mixed_dot(left, right, dims=(((1,), (0,)), ((), ())), count=3):
    total = None
    for part in reversed(pieces(left, count)):
        term = lax.dot_general(part, right, dims, preferred_element_type=F32)
        total = term if total is None else total + term
    return total


def turn_kernel(mask_ref, u_ref, t_ref):
    chunk = pl.program_id(0)
    tall, steps, width, _ = u_ref.shape
    for a in range(tall):
        for k in range(steps):
            row = chunk * tall + a
            block = jnp.where(mask_ref[row, k] > 0, u_ref[a, k].astype(F32), 0.0)
            t_ref[k * width : (k + 1) * width, a * width : (a + 1) * width] = block.T.astype(BF16)


def turned(lower, mask, tall):
    row_blocks, steps, width, _ = lower.shape
    chunks = row_blocks // tall
    return pl.pallas_call(
        turn_kernel,
        grid=(chunks,),
        in_specs=[
            pl.BlockSpec(memory_space=pltpu.SMEM),
            pl.BlockSpec((tall, steps, width, width), lambda k: (k, 0, 0, 0)),
        ],
        out_specs=pl.BlockSpec((None, steps * width, tall * width), lambda k: (k, 0, 0)),
        out_shape=jax.ShapeDtypeStruct((chunks, steps * width, tall * width), BF16),
        compiler_params=pltpu.CompilerParams(vmem_limit_bytes=40 << 20),
    )(mask, lower)


def product_kernel(x_ref, u_ref, *rest):
    o_ref, y_ref, acc_ref = rest[-3:]
    k = pl.program_id(1)
    tall, group, width, _ = x_ref.shape
    o_ref[...] = x_ref[...]
    tile = jnp.concatenate([x_ref[:, g].reshape(tall * width, width) for g in range(group)], axis=1)
    high, low = pieces(tile, 2)
    left = u_ref[k]
    part = jnp.dot(left, low, preferred_element_type=F32) + jnp.dot(left, high, preferred_element_type=F32)

    @pl.when(k == 0)
    def _():
        acc_ref[...] = part

    @pl.when(k > 0)
    def _():
        acc_ref[...] += part

    @pl.when(k == pl.num_programs(1) - 1)
    def _():
        y_ref[...] = acc_ref[...].T


def product(blocks, left, copied, start, count):
    row_blocks, _, width, _ = blocks.shape
    chunks, depth, length = left.shape
    group = 2 if count % 2 == 0 else 1
    tall = length // width
    place = pl.BlockSpec((tall, group, width, width), lambda c, k: (k, start // group + c, 0, 0))
    operands = [blocks, left]
    in_specs = [
        place,
        pl.BlockSpec(left.shape, lambda c, k: (0, 0, 0), pipeline_mode=pl.Buffered(1)),
    ]
    aliases = {}
    if copied is not None:
        operands.append(copied)
        in_specs.append(pl.BlockSpec(memory_space=pl.ANY))
        aliases = {2: 0}
    return pl.pallas_call(
        product_kernel,
        grid=(count // group, chunks),
        in_specs=in_specs,
        out_specs=[place, pl.BlockSpec((group * width, depth), lambda c, k: (c, 0))],
        out_shape=[
            jax.ShapeDtypeStruct(blocks.shape, F32),
            jax.ShapeDtypeStruct((count * width, depth), F32),
        ],
        scratch_shapes=[pltpu.VMEM((depth, group * width), F32)],
        input_output_aliases=aliases,
        compiler_params=pltpu.CompilerParams(vmem_limit_bytes=56 << 20),
        cost_estimate=pl.CostEstimate(
            flops=4 * row_blocks * count * width**2 * depth,
            bytes_accessed=8 * row_blocks * count * width**2,
            transcendentals=0,
        ),
    )(*operands)


def write_kernel(flag_ref, col_ref, row_ref, x_ref, o_ref, sem):
    slots = row_ref.shape[0]

    @pl.when(flag_ref[0] > 0)
    def _():
        copy = pltpu.make_async_copy(col_ref, o_ref.at[:, 0], sem.at[0])
        copy.start()
        copy.wait()

    for slot in range(slots):

        @pl.when(flag_ref[1 + slot] > 0)
        def _():
            copy = pltpu.make_async_copy(row_ref.at[slot], o_ref.at[slot], sem.at[1 + slot])
            copy.start()
            copy.wait()


def write(flags, new_col, new_rows, copied):
    slots = new_rows.shape[0]
    return pl.pallas_call(
        write_kernel,
        in_specs=[
            pl.BlockSpec(memory_space=pltpu.SMEM),
            pl.BlockSpec(memory_space=pltpu.VMEM),
            pl.BlockSpec(memory_space=pltpu.VMEM),
            pl.BlockSpec(memory_space=pl.ANY),
        ],
        out_specs=pl.BlockSpec(memory_space=pl.ANY),
        out_shape=jax.ShapeDtypeStruct(copied.shape, F32),
        scratch_shapes=[pltpu.SemaphoreType.DMA((1 + slots,))],
        input_output_aliases={3: 0},
        compiler_params=pltpu.CompilerParams(vmem_limit_bytes=40 << 20),
    )(flags, new_col, new_rows, copied)


def packed(j, k):
    return j * (j + 1) // 2 + k


def substitute_kernel(steps, y_ref, mask_ref, small_ref, rows_ref, z_ref, p_ref):
    width = y_ref.shape[1] // steps
    for k in reversed(range(steps)):
        here = slice(k * width, (k + 1) * width)
        value = y_ref[:, here]
        if k + 1 < steps:
            later = slice((k + 1) * width, steps * width)
            value = value + mixed_dot(z_ref[:, later], small_ref[later, here])
        z_ref[:, here] = jnp.where(mask_ref[:, k : k + 1] > 0, -value, 0.0)
    for j in range(steps):
        upto = slice(0, (j + 1) * width)
        there = slice(j * width, (j + 1) * width)
        value = mixed_dot(z_ref[:, there], rows_ref[:, upto], (((0,), (0,)), ((), ())))
        for k in range(j + 1):
            p_ref[packed(j, k)] = value[:, k * width : (k + 1) * width]


def corner_kernel(steps, p_ref, small_ref, dinv_ref, mask_ref, s_ref):
    width = dinv_ref.shape[1]
    for k in reversed(range(steps)):
        here = slice(k * width, (k + 1) * width)
        diag = dinv_ref[k] - p_ref[packed(k, k)].T
        if k + 1 < steps:
            later = slice((k + 1) * width, steps * width)
            factor = small_ref[later, here]
            known = jnp.concatenate([p_ref[packed(j, k)] for j in range(k + 1, steps)], axis=0)
            value = known + mixed_dot(s_ref[later, later], factor)
            value = jnp.where(mask_ref[later, k : k + 1] > 0, -value, 0.0)
            diag = diag - mixed_dot(value, factor, (((0,), (0,)), ((), ()))).T
            s_ref[later, here] = value
            s_ref[here, later] = value.T
        s_ref[here, here] = diag.T


def per_device(ainv_in, ufactor, dinv, pattern):
    row_blocks, _, col_blocks, _, width, _ = ainv_in.shape
    steps = dinv.shape[0]
    blocks = ainv_in.reshape(row_blocks, col_blocks, width, width)
    lower = ufactor.reshape(row_blocks, steps, width, width)
    row_count = lax.axis_size("prow")
    col_count = lax.axis_size("pcol")
    prow_id = lax.axis_index("prow")
    pcol_id = lax.axis_index("pcol")
    fold = col_count // row_count
    slots = -(-steps // row_count)
    assert slots <= fold and steps <= col_count
    row_ids = jnp.arange(row_blocks, dtype=jnp.int32) * row_count + prow_id
    col_ids = jnp.arange(col_blocks, dtype=jnp.int32) * col_count + pcol_id

    heads = pattern[:, :steps]
    row_pattern = lax.dynamic_index_in_dim(heads.reshape(row_blocks, row_count, steps), prow_id, 1, keepdims=False)
    col_pattern = lax.dynamic_index_in_dim(heads.reshape(col_blocks, col_count, steps), pcol_id, 1, keepdims=False)
    outer_rows = jnp.where((row_ids >= steps)[:, None], row_pattern, 0)
    outer_cols = jnp.where((col_ids >= steps)[:, None], col_pattern, 0)

    heads_live = row_pattern[:slots] > 0
    small = jnp.where(heads_live[:, :, None, None], lower[:slots], jnp.zeros_like(lower[:slots]))
    small = lax.all_gather(small, "prow", axis=1)
    small = small.reshape(slots * row_count, steps, width, width)[:steps]
    small = small.transpose(0, 2, 1, 3).reshape(steps * width, steps * width)

    chosen = lax.dynamic_index_in_dim(
        lower.reshape(col_blocks, fold, steps, width, width), pcol_id // row_count, 1, keepdims=False
    )
    at_home = (outer_cols > 0) & (prow_id == pcol_id % row_count)
    chosen = jnp.where(at_home[:, :, None, None], chosen, jnp.zeros_like(chosen))
    chosen = chosen.transpose(0, 2, 1, 3).reshape(col_blocks * width, steps * width)

    left = turned(lower, outer_rows, largest_divisor(row_blocks, 9))
    parts = 3 if col_blocks % 3 == 0 else 1
    count = col_blocks // parts
    span = count * width
    share = span // row_count
    mask_all = jnp.repeat(outer_cols.astype(F32), width, axis=0)
    params = pltpu.CompilerParams(vmem_limit_bytes=40 << 20)
    triangle = steps * (steps + 1) // 2
    copied, products, mine_parts, received_parts = None, None, [], []
    for part in range(parts):
        copied, partial_y = product(blocks, left, copied, part * count, count)
        here = slice(part * span, (part + 1) * span)
        factor_rows = lax.psum_scatter(chosen[here], "prow", scatter_dimension=0, tiled=True)
        share_y = lax.psum_scatter(partial_y, "prow", scatter_dimension=0, tiled=True)
        mask_rows = lax.dynamic_slice_in_dim(mask_all[here], prow_id * share, share, 0)
        share_z, product_part = pl.pallas_call(
            functools.partial(substitute_kernel, steps),
            out_shape=[
                jax.ShapeDtypeStruct(share_y.shape, F32),
                jax.ShapeDtypeStruct((triangle, width, width), F32),
            ],
            compiler_params=params,
        )(share_y, mask_rows, small, factor_rows)
        products = product_part if products is None else products + product_part

        padded = jnp.pad(share_z, ((0, 0), (0, (slots * row_count - steps) * width)))
        padded = padded.reshape(share, slots, row_count, width)
        mine = lax.all_to_all(padded, "prow", split_axis=2, concat_axis=0, tiled=True)
        mine = mine.reshape(count, width, slots, width)
        mine_parts.append(mine)

        received = []
        for turn in range(fold):
            pairs = []
            for slot in range(slots):
                side = (turn + slot) % fold
                for p in range(row_count):
                    if slot * row_count + p < steps:
                        for r in range(row_count):
                            source = p * col_count + side * row_count + r
                            target = r * col_count + slot * row_count + p
                            pairs.append((source, target))
            slot = jnp.minimum((pcol_id // row_count + fold - turn) % fold, slots - 1)
            payload = lax.dynamic_index_in_dim(mine, slot, 2, keepdims=False)
            received.append(lax.ppermute(payload, ("prow", "pcol"), pairs))
        received_parts.append(jnp.stack(received))
    products = lax.psum(products, ("prow", "pcol"))
    mine = jnp.concatenate(mine_parts, axis=0)
    stacked = jnp.concatenate(received_parts, axis=1)

    mask_small = jnp.repeat(pattern[:steps, :steps].astype(F32), width, axis=0)
    corner = pl.pallas_call(
        functools.partial(corner_kernel, steps),
        out_shape=jax.ShapeDtypeStruct((steps * width, steps * width), F32),
        compiler_params=params,
    )(products, small, dinv, mask_small)
    corner = corner.reshape(steps, width, steps, width)

    my_slot = pcol_id // row_count
    new_col = jnp.stack([stacked[(side - my_slot) % fold] for side in range(fold)], axis=1)
    new_col = new_col.reshape(row_blocks, width, width)
    own = jnp.minimum(pcol_id, steps - 1)
    corner_col = lax.dynamic_index_in_dim(corner, own, 2, keepdims=False)
    for slot in range(slots):
        index = slot * row_count + prow_id
        block = lax.dynamic_index_in_dim(corner_col, jnp.minimum(index, steps - 1), 0, keepdims=False)
        new_col = new_col.at[slot].set(jnp.where(index < steps, block, new_col[slot]))
    new_rows, flags = [], [pcol_id < steps]
    for slot in range(slots):
        index = slot * row_count + prow_id
        new_row = jnp.swapaxes(mine[:, :, slot], 1, 2)
        block = lax.dynamic_index_in_dim(corner, jnp.minimum(index, steps - 1), 0, keepdims=False)
        block = lax.dynamic_index_in_dim(block, own, 1, keepdims=False)
        new_rows.append(new_row.at[0].set(jnp.where(pcol_id < steps, block, new_row[0])))
        flags.append(index < steps)
    matrix = write(jnp.stack(flags).astype(jnp.int32), new_col, jnp.stack(new_rows), copied)
    return matrix.reshape(ainv_in.shape)


def solution(mesh):
    placed = (
        P(None, "prow", None, "pcol", None, None),
        P(None, "prow", None, None, None),
        P(),
        P(),
    )
    return jax.shard_map(
        per_device,
        mesh=mesh,
        in_specs=placed,
        out_specs=P(None, "prow", None, "pcol", None, None),
        check_vma=False,
    )
```
